512 devices in a mesh: dp: 32 (over x_hi, z, core), mp: 16 (over x_lo, y).
Axes of the slice: x: 4 (x_hi: 2, x_lo: 2; x = x_hi * 2 + x_lo), y: 8, z: 8, core: 2. Of those that a mesh axis runs over, the one named last changes fastest.
Arguments:
- tokens: bfloat16 [8192, 6144], P('dp', 'mp'), may hold values from -6 to 6
- grad_act: bfloat16 [8192, 24576], P('dp', 'mp'), may hold values from -6 to 6
- weight_blocks: bfloat16 [1024, 128, 128], P('mp'), may hold values from -0.21875 to 0.21875
- block_rows: int32 [1024], P('mp'), may hold values from 0 to 47
- block_cols: int32 [1024], P('mp'), may hold values from 0 to 11
- block_counts: int32 [16], P('mp'), may hold values from 48 to 64, as said below
Outputs:
- activated: bfloat16 [8192, 24576], P('dp', 'mp')
- grad_input: bfloat16 [8192, 6144], P('dp', 'mp')
- grad_blocks: float32 [1024, 128, 128], P('mp', 'dp')
The draws below stay inside these ranges and needn't reach their ends.
Inputs may be any that keep to these rules, and one draw needn't show every extreme that they name: `block_counts`: within one holder the filled slots name distinct cells (block row, block column); one holder has all 64 slots filled in every draw.
All inputs are finite; a program needn't handle non-finite values.
Results may differ from the reference program's by a relative error of at most 0.019.
Values may be sent and summed in bfloat16 or wider, within the bound.
No kernel may reach another device: no remote copies, remote signals or barrier semaphores. Data moves between devices by JAX's collectives and lax.ppermute only.
A program may use at most 64 MiB of HBM per device.

```python
import jax
import jax.numpy as jnp
from jax import lax

D = 6144
FF = 24576
BS = 128
SPARSITY = 9
TOK_DEV = 256
TOKENS = 8192
HOLDERS = 16
ROW_BLOCKS = 48
COLS_DEV = 12
MAXB = 64
N_DP = 32


def block_cells(key):
    holder_keys = jax.random.split(jax.random.fold_in(key, 7), HOLDERS)
    cell_total = ROW_BLOCKS * COLS_DEV

    def one_holder(holder_key):
        return jax.random.permutation(holder_key, cell_total)[:MAXB]
    chosen = jax.vmap(one_holder)(holder_keys).astype(jnp.int32)
    return chosen.reshape(HOLDERS * MAXB)


def draw_block_rows(key, part):
    return (block_cells(key) // COLS_DEV).astype(jnp.int32)


def draw_block_cols(key, part):
    return (block_cells(key) % COLS_DEV).astype(jnp.int32)


def draw_block_counts(key, part):
    lowest = MAXB - MAXB // 4
    filled = jax.random.randint(jax.random.fold_in(key, 11), (HOLDERS,), lowest, MAXB + 1)
    fullest = jax.random.randint(jax.random.fold_in(key, 13), (), 0, HOLDERS)
    positions = jnp.arange(HOLDERS, dtype=jnp.int32)
    return jnp.where(positions == fullest, MAXB, filled).astype(jnp.int32)


def block_scale(key, dims, cuts, least, top_value):
    level = 1.0
    for axis_at, blocks in cuts:
        steps = jax.random.uniform(jax.random.fold_in(jax.random.fold_in(key, 6), axis_at), (blocks,), jnp.float32, least / len(cuts), top_value / len(cuts))
        level = level * jnp.repeat(jnp.exp(steps), dims[axis_at] // blocks).reshape((-1,) + (1,) * (len(dims) - 1 - axis_at))
    return level


def bell_draw(own_key, shape, spread, reach, cuts=(), held_as=jnp.bfloat16):
    entries = spread * jax.random.normal(own_key, shape, jnp.float32)
    if cuts:
        entries = entries * block_scale(own_key, shape, cuts, -0.22, 0.18)
    return jnp.clip(entries, -reach, reach).astype(held_as)


def setup_inputs(seed: int = 0) -> dict:
    keys = jax.random.split(jax.random.key(seed), 7)
    tokens = bell_draw(keys[0], (TOKENS, D), 1.0, 6.0, ((0, 32), (1, 16)))
    grad_act = bell_draw(keys[1], (TOKENS, FF), 1.0, 6.0, ((0, 32), (1, 16)))
    weight_blocks = bell_draw(keys[2], (HOLDERS * MAXB, BS, BS), (D // SPARSITY) ** -0.5, 0.21875, ((0, 16),))
    block_rows = draw_block_rows(jax.random.fold_in(keys[6], 71), 0)
    block_cols = draw_block_cols(jax.random.fold_in(keys[6], 71), 0)
    block_counts = draw_block_counts(jax.random.fold_in(keys[6], 71), 0)
    return {"tokens": tokens, "grad_act": grad_act, "weight_blocks": weight_blocks, "block_rows": block_rows, "block_cols": block_cols, "block_counts": block_counts}


inv_sqrt_two = 0.7071067811865476
inv_sqrt_two_pi = 0.3989422804014327

def gelu_pair(preact):
    normal_cdf = 0.5 * (1.0 + lax.erf(preact * inv_sqrt_two))
    activated = preact * normal_cdf
    slopes = normal_cdf + preact * jnp.exp(-0.5 * preact * preact) * inv_sqrt_two_pi
    return (activated, slopes)

def reference(tokens, grad_act, weight_blocks, block_rows, block_cols, block_counts):
    tok_blocks = tokens.reshape(TOKENS, ROW_BLOCKS, BS)
    grad_holders = jnp.transpose(grad_act.reshape(TOKENS, HOLDERS, COLS_DEV, BS), (1, 0, 2, 3))
    weight_holders = weight_blocks.reshape(HOLDERS, MAXB, BS, BS)
    row_table = block_rows.reshape(HOLDERS, MAXB)
    col_table = block_cols.reshape(HOLDERS, MAXB)

    def advance(carried, inputs_now):
        weights, row_ids, col_ids, filled, grad_here = inputs_now
        slot_live = (jnp.arange(MAXB, dtype=jnp.int32) < filled).astype(jnp.float32)
        slot_tokens = jnp.take(tok_blocks, row_ids, axis=1)
        weights_wide = weights.astype(jnp.float32)
        products = jnp.einsum('tsk,skn->tsn', slot_tokens.astype(jnp.float32), weights_wide)
        col_hot = (col_ids[:, None] == jnp.arange(COLS_DEV, dtype=jnp.int32)[None, :]).astype(jnp.float32) * slot_live[:, None]
        preact = jnp.einsum('tsn,sc->tcn', products, col_hot, precision=lax.Precision.HIGHEST)
        activated, slopes = gelu_pair(preact)
        grad_pre = (grad_here.astype(jnp.float32) * slopes).astype(jnp.bfloat16)
        grad_slots = jnp.take(grad_pre, col_ids, axis=1)
        backward = jnp.einsum('tsn,skn->tsk', grad_slots.astype(jnp.float32), weights_wide) * slot_live[None, :, None]
        row_hot = (row_ids[:, None] == jnp.arange(ROW_BLOCKS, dtype=jnp.int32)[None, :]).astype(jnp.float32)
        partial_value = jnp.einsum('tsk,sr->trk', backward, row_hot, precision=lax.Precision.HIGHEST).astype(jnp.bfloat16)
        partial_value = lax.optimization_barrier(partial_value).astype(jnp.float32)
        group_tokens = slot_tokens.reshape(N_DP, TOK_DEV, MAXB, BS).astype(jnp.float32)
        group_grads = grad_slots.reshape(N_DP, TOK_DEV, MAXB, BS).astype(jnp.float32)
        group_parts = jnp.einsum('gtsk,gtsn->gskn', group_tokens, group_grads) * slot_live[None, :, None, None]
        group_parts = lax.optimization_barrier(group_parts.astype(jnp.bfloat16)).astype(jnp.float32)
        grad_here_blocks = lax.optimization_barrier(jnp.sum(group_parts, axis=0))
        return (carried + partial_value, (activated.astype(jnp.bfloat16), grad_here_blocks))
    start_sum = jnp.zeros((TOKENS, ROW_BLOCKS, BS), jnp.float32)
    total, outputs = lax.scan(advance, start_sum, (weight_holders, row_table, col_table, block_counts, grad_holders))
    act_holders, grad_holder_blocks = outputs
    activated = jnp.transpose(act_holders, (1, 0, 2, 3)).reshape(TOKENS, FF)
    grad_input = total.reshape(TOKENS, D).astype(jnp.bfloat16)
    grad_blocks = grad_holder_blocks.reshape(HOLDERS * MAXB, BS, BS)
    return (activated, grad_input, grad_blocks)
```

```python
import functools

import jax
import jax.numpy as jnp
from jax import lax
from jax.experimental import pallas as pl
from jax.experimental.pallas import tpu as pltpu
from jax.sharding import Mesh, PartitionSpec as P


inv_sqrt_two = 0.7071067811865476
inv_sqrt_two_pi = 0.3989422804014327

AXES = ("xh", "z", "core", "xl", "y")
SIZES = (2, 8, 2, 2, 8)
DP = ("xh", "z", "core")
MP = ("xl", "y")
NEAR = SIZES[3]
FAR = SIZES[4]
UNROLL = 4


def cols_at(block, side):
    return (slice(None), pl.ds(pl.multiple_of(block * side, side), side))


def row_at(row, per, side):
    holder = row // per
    place = (holder % FAR) * NEAR + holder // FAR
    return (place,) + cols_at(row % per, side)


def hidden_kernel(rows, cols, count, x_ref, g_ref, w_ref, act_ref, gpre_ref, gin_ref, pre, acc):
    slots, side = w_ref.shape[0], w_ref.shape[1]
    tok, per = x_ref.shape[1], x_ref.shape[2] // side
    live = count[0]

    def weight(s):
        block = w_ref[s]
        return jnp.where(s < live, block, jnp.zeros_like(block))

    pre[...] = jnp.zeros_like(pre)

    @pl.loop(0, slots // UNROLL)
    def _(group):
        products = []
        for k in range(UNROLL):
            s = group * UNROLL + k
            products.append(
                jnp.dot(
                    x_ref[row_at(rows[s], per, side)],
                    weight(s),
                    preferred_element_type=jnp.float32,
                )
            )
        for k in range(UNROLL):
            pre[cols_at(cols[group * UNROLL + k], side)] += products[k]

    step = 16

    @pl.loop(0, tok // step)
    def _(i):
        at = (pl.ds(pl.multiple_of(i * step, step), step), slice(None))
        v = pre[at]
        normal_cdf = 0.5 * (1.0 + lax.erf(v * inv_sqrt_two))
        act_ref[at] = (v * normal_cdf).astype(jnp.bfloat16)
        slopes = normal_cdf + v * jnp.exp(-0.5 * v * v) * inv_sqrt_two_pi
        gpre_ref[at] = (g_ref[at].astype(jnp.float32) * slopes).astype(jnp.bfloat16)

    acc[...] = jnp.zeros_like(acc)

    @pl.loop(0, slots // UNROLL)
    def _(group):
        products = []
        for k in range(UNROLL):
            s = group * UNROLL + k
            products.append(
                lax.dot_general(
                    gpre_ref[cols_at(cols[s], side)],
                    weight(s),
                    (((1,), (1,)), ((), ())),
                    preferred_element_type=jnp.float32,
                )
            )
        for k in range(UNROLL):
            acc[row_at(rows[group * UNROLL + k], per, side)] += products[k]

    gin_ref[...] = acc[...].astype(jnp.bfloat16)


def hidden(x, grad_act, weight_blocks, rows, cols, count):
    holders, tok, width = x.shape
    ff = grad_act.shape[1]
    slots, side, _ = weight_blocks.shape
    vmem = pl.BlockSpec(memory_space=pltpu.VMEM)
    return pl.pallas_call(
        hidden_kernel,
        grid_spec=pltpu.PrefetchScalarGridSpec(
            num_scalar_prefetch=3,
            grid=(),
            in_specs=[vmem] * 3,
            out_specs=[vmem] * 3,
            scratch_shapes=[
                pltpu.VMEM((tok, ff), jnp.float32),
                pltpu.VMEM((holders, tok, width), jnp.float32),
            ],
        ),
        out_shape=[
            jax.ShapeDtypeStruct((tok, ff), jnp.bfloat16),
            jax.ShapeDtypeStruct((tok, ff), jnp.bfloat16),
            jax.ShapeDtypeStruct((holders, tok, width), jnp.bfloat16),
        ],
        compiler_params=pltpu.CompilerParams(vmem_limit_bytes=32 * 2**20),
        cost_estimate=pl.CostEstimate(
            flops=4 * slots * tok * side * side,
            bytes_accessed=12 * 2**20,
            transcendentals=2 * tok * ff,
        ),
        name="hidden",
    )(rows, cols, count, x, grad_act, weight_blocks)


def blocks_kernel(rows, cols, count, core_ref, x_ref, gpre_ref, keep_ref, send_ref):
    side = gpre_ref.shape[0] // 2
    slots = rows.shape[0]
    per = x_ref.shape[2] // side
    live = count[0]
    groups = keep_ref.shape[0]
    to = lax.broadcasted_iota(jnp.int32, (2 * side, 2 * side), 0)
    source = lax.broadcasted_iota(jnp.int32, (2 * side, 2 * side), 1)
    core = (to // side + core_ref[0]) % 2
    wanted = ((to % 8) // 4) * side + ((to % side) // 8 * 2 + core) * 4 + to % 4
    pick = (source == wanted).astype(jnp.float32).astype(jnp.bfloat16)

    @pl.loop(0, slots // UNROLL)
    def _(group):
        for h in range(UNROLL // 2):
            pair = []
            for k in range(2):
                s = group * UNROLL + h * 2 + k
                value = lax.dot_general(
                    x_ref[row_at(rows[s], per, side)],
                    gpre_ref[cols_at(cols[s], side)],
                    (((0,), (0,)), ((), ())),
                    preferred_element_type=jnp.float32,
                )
                pair.append(jnp.where(s < live, value, 0.0).astype(jnp.bfloat16))
            both = jnp.dot(pick, jnp.concatenate(pair, 0), preferred_element_type=jnp.float32)
            both = both.astype(jnp.bfloat16).reshape(2, groups, 8, side)
            keep_ref[:, group * (UNROLL // 2) + h] = both[0]
            send_ref[:, group * (UNROLL // 2) + h] = both[1]


def blocks(x, grad_pre, rows, cols, count, core):
    slots = rows.shape[0]
    tok = x.shape[1]
    side = tok // 2
    half = jax.ShapeDtypeStruct((SIZES[0] * SIZES[1], slots // 2, 8, side), jnp.bfloat16)
    vmem = pl.BlockSpec(memory_space=pltpu.VMEM)
    return pl.pallas_call(
        blocks_kernel,
        grid_spec=pltpu.PrefetchScalarGridSpec(
            num_scalar_prefetch=4,
            grid=(),
            in_specs=[vmem] * 2,
            out_specs=[vmem] * 2,
        ),
        out_shape=[half, half],
        compiler_params=pltpu.CompilerParams(vmem_limit_bytes=24 * 2**20),
        cost_estimate=pl.CostEstimate(
            flops=8 * slots * tok * side * side, bytes_accessed=8 * 2**20, transcendentals=0
        ),
        name="blocks",
    )(rows, cols, count, core, x, grad_pre)


def shards(tokens, grad_act, weight_blocks, block_rows, block_cols, block_counts):
    tok, width = tokens.shape
    slots = weight_blocks.shape[0]
    near = lax.all_gather(tokens, "xl", axis=0, tiled=False)
    whole = lax.all_gather(near, "y", axis=0, tiled=False).reshape(FAR * NEAR, tok, width)
    activated, grad_pre, input_partial = hidden(
        whole, grad_act, weight_blocks, block_rows, block_cols, block_counts
    )

    far_sum = lax.psum_scatter(
        input_partial.reshape(FAR, NEAR, tok, width), "y", scatter_dimension=0, tiled=True
    )[0]
    place = lax.axis_index("xl")
    kept = lax.dynamic_index_in_dim(far_sum, place, 0, keepdims=False)
    given = lax.dynamic_index_in_dim(far_sum, 1 - place, 0, keepdims=False)
    both = lax.all_gather(given, "xl", axis=0, tiled=False)
    taken = lax.dynamic_index_in_dim(both, 1 - place, 0, keepdims=False)
    grad_input = (kept.astype(jnp.float32) + taken.astype(jnp.float32)).astype(jnp.bfloat16)

    core = lax.axis_index("core").astype(jnp.int32).reshape(1)
    keep, send = blocks(whole, grad_pre, block_rows, block_cols, block_counts, core)
    other = lax.ppermute(send, "core", [(0, 1), (1, 0)])
    chip_sum = (keep.astype(jnp.float32) + other.astype(jnp.float32)).astype(jnp.bfloat16)
    parts = lax.all_to_all(chip_sum, ("xh", "z"), split_axis=0, concat_axis=0, tiled=True)
    grad_blocks = jnp.sum(parts.astype(jnp.float32), axis=0)
    return (activated, grad_input, grad_blocks.reshape(slots, 4, grad_blocks.shape[-1]))


def solution(mesh):
    cut = Mesh(mesh.devices.reshape(SIZES), AXES)
    placed = (P(DP, MP), P(DP, MP), P(MP, None, None), P(MP), P(MP), P(MP))
    return jax.shard_map(
        shards,
        mesh=cut,
        in_specs=placed,
        out_specs=(P(DP, MP), P(DP, MP), P(MP, DP, None)),
        check_vma=False,
    )
```

```python
import functools

import jax
import jax.numpy as jnp
from jax import lax
from jax.experimental import pallas as pl
from jax.experimental.pallas import tpu as pltpu
from jax.sharding import Mesh, PartitionSpec as P


inv_sqrt_two = 0.7071067811865476
inv_sqrt_two_pi = 0.3989422804014327

AXES = ("xh", "z", "core", "xl", "y")
SIZES = (2, 8, 2, 2, 8)
DP = ("xh", "z", "core")
MP = ("xl", "y")
NEAR = SIZES[3]
FAR = SIZES[4]
UNROLL = 4


def cols_at(block, side):
    return (slice(None), pl.ds(pl.multiple_of(block * side, side), side))


def row_at(place, part, side):
    return (place,) + cols_at(part, side)


FROM, TO, PART, COL, LIVE, CORE = range(6)


def index_table(block_rows, block_cols, block_counts, per):
    holder = block_rows // per
    own = lax.axis_index("xl").astype(jnp.int32)
    start = (holder % FAR) * NEAR
    near = holder // FAR
    live = (jnp.arange(block_rows.shape[0], dtype=jnp.int32) < block_counts[0]).astype(jnp.int32)
    core = jnp.broadcast_to(lax.axis_index("core").astype(jnp.int32), block_rows.shape)
    return jnp.stack(
        [start + near, start + (near + own) % NEAR, block_rows % per, block_cols, live, core]
    )


def hidden_kernel(
    table,
    x_hbm,
    g_hbm,
    w_hbm,
    act_hbm,
    gpre_hbm,
    gin_hbm,
    x_ref,
    g_ref,
    w_ref,
    act_ref,
    gpre_ref,
    gin_ref,
    pre,
    acc,
    x_sem,
    gin_sem,
    g_sem,
    w_sem,
    act_sem,
    gpre_sem,
):
    slots, side = w_ref.shape[0], w_ref.shape[1]
    holders, tok = x_ref.shape[0], x_ref.shape[1]

    def x_copy(i):
        return pltpu.make_async_copy(x_hbm.at[i], x_ref.at[i], x_sem.at[i])

    def gin_copy(i):
        return pltpu.make_async_copy(gin_ref.at[i], gin_hbm.at[i], gin_sem.at[i])

    g_copy = pltpu.make_async_copy(g_hbm, g_ref, g_sem)
    w_copy = pltpu.make_async_copy(w_hbm, w_ref, w_sem)
    act_copy = pltpu.make_async_copy(act_ref, act_hbm, act_sem)
    gpre_copy = pltpu.make_async_copy(gpre_ref, gpre_hbm, gpre_sem)

    w_copy.start()

    @pl.loop(0, holders)
    def _(i):
        x_copy(i).start()

    g_copy.start()
    pre[...] = jnp.zeros_like(pre)
    acc[...] = jnp.zeros_like(acc)
    w_copy.wait()

    @pl.loop(0, holders)
    def _(i):
        x_copy(i).wait()

    @pl.loop(0, slots // UNROLL)
    def _(group):
        products = []
        for k in range(UNROLL):
            s = group * UNROLL + k
            products.append(
                jnp.dot(
                    x_ref[row_at(table[FROM, s], table[PART, s], side)],
                    w_ref[s],
                    preferred_element_type=jnp.float32,
                )
            )
        for k in range(UNROLL):
            pre[cols_at(table[COL, group * UNROLL + k], side)] += products[k]

    g_copy.wait()
    step = 16

    @pl.loop(0, tok // step)
    def _(i):
        at = (pl.ds(pl.multiple_of(i * step, step), step), slice(None))
        v = pre[at]
        normal_cdf = 0.5 * (1.0 + lax.erf(v * inv_sqrt_two))
        act_ref[at] = (v * normal_cdf).astype(jnp.bfloat16)
        slopes = normal_cdf + v * jnp.exp(-0.5 * v * v) * inv_sqrt_two_pi
        gpre_ref[at] = (g_ref[at].astype(jnp.float32) * slopes).astype(jnp.bfloat16)

    act_copy.start()
    gpre_copy.start()

    @pl.loop(0, slots // UNROLL)
    def _(group):
        products = []
        for k in range(UNROLL):
            s = group * UNROLL + k
            products.append(
                lax.dot_general(
                    gpre_ref[cols_at(table[COL, s], side)],
                    w_ref[s],
                    (((1,), (1,)), ((), ())),
                    preferred_element_type=jnp.float32,
                )
            )
        for k in range(UNROLL):
            s = group * UNROLL + k
            acc[row_at(table[TO, s], table[PART, s], side)] += products[k]

    @pl.loop(0, holders)
    def _(i):
        gin_ref[i] = acc[i].astype(jnp.bfloat16)
        gin_copy(i).start()

    act_copy.wait()
    gpre_copy.wait()

    @pl.loop(0, holders)
    def _(i):
        gin_copy(i).wait()


def hidden(x, grad_act, weights, table):
    holders, tok, width = x.shape
    ff = grad_act.shape[1]
    slots, side, _ = weights.shape
    hbm = pl.BlockSpec(memory_space=pltpu.HBM)
    narrow = jnp.bfloat16
    return pl.pallas_call(
        hidden_kernel,
        grid_spec=pltpu.PrefetchScalarGridSpec(
            num_scalar_prefetch=1,
            grid=(),
            in_specs=[hbm] * 3,
            out_specs=[hbm] * 3,
            scratch_shapes=[
                pltpu.VMEM((holders, tok, width), narrow),
                pltpu.VMEM((tok, ff), narrow),
                pltpu.VMEM((slots, side, side), narrow),
                pltpu.VMEM((tok, ff), narrow),
                pltpu.VMEM((tok, ff), narrow),
                pltpu.VMEM((holders, tok, width), narrow),
                pltpu.VMEM((tok, ff), jnp.float32),
                pltpu.VMEM((holders, tok, width), jnp.float32),
                pltpu.SemaphoreType.DMA((holders,)),
                pltpu.SemaphoreType.DMA((holders,)),
                pltpu.SemaphoreType.DMA,
                pltpu.SemaphoreType.DMA,
                pltpu.SemaphoreType.DMA,
                pltpu.SemaphoreType.DMA,
            ],
        ),
        out_shape=[
            jax.ShapeDtypeStruct((tok, ff), narrow),
            jax.ShapeDtypeStruct((tok, ff), narrow),
            jax.ShapeDtypeStruct((holders, tok, width), narrow),
        ],
        compiler_params=pltpu.CompilerParams(vmem_limit_bytes=60 * 2**20),
        cost_estimate=pl.CostEstimate(
            flops=4 * slots * tok * side * side,
            bytes_accessed=12 * 2**20,
            transcendentals=2 * tok * ff,
        ),
        name="hidden",
    )(table, x, grad_act, weights)


def blocks_kernel(table, x_ref, gpre_ref, keep_ref, send_ref):
    side = gpre_ref.shape[0] // 2
    slots = table.shape[1]
    groups = keep_ref.shape[0]
    to = lax.broadcasted_iota(jnp.int32, (2 * side, 2 * side), 0)
    source = lax.broadcasted_iota(jnp.int32, (2 * side, 2 * side), 1)
    core = (to // side + table[CORE, 0]) % 2
    wanted = ((to % 8) // 4) * side + ((to % side) // 8 * 2 + core) * 4 + to % 4
    pick = (source == wanted).astype(jnp.float32).astype(jnp.bfloat16)

    @pl.loop(0, slots // UNROLL)
    def _(group):
        for h in range(UNROLL // 2):
            pair = []
            for k in range(2):
                s = group * UNROLL + h * 2 + k
                value = lax.dot_general(
                    x_ref[row_at(table[FROM, s], table[PART, s], side)],
                    gpre_ref[cols_at(table[COL, s], side)],
                    (((0,), (0,)), ((), ())),
                    preferred_element_type=jnp.float32,
                )
                pair.append(jnp.where(table[LIVE, s] > 0, value, 0.0).astype(jnp.bfloat16))
            both = jnp.dot(pick, jnp.concatenate(pair, 0), preferred_element_type=jnp.float32)
            both = both.astype(jnp.bfloat16).reshape(2, groups, 8, side)
            keep_ref[:, group * (UNROLL // 2) + h] = both[0]
            send_ref[:, group * (UNROLL // 2) + h] = both[1]


def blocks(x, grad_pre, table):
    slots = table.shape[1]
    tok = x.shape[1]
    side = tok // 2
    half = jax.ShapeDtypeStruct((SIZES[0] * SIZES[1], slots // 2, 8, side), jnp.bfloat16)
    vmem = pl.BlockSpec(memory_space=pltpu.VMEM)
    return pl.pallas_call(
        blocks_kernel,
        grid_spec=pltpu.PrefetchScalarGridSpec(
            num_scalar_prefetch=1,
            grid=(),
            in_specs=[vmem] * 2,
            out_specs=[vmem] * 2,
        ),
        out_shape=[half, half],
        compiler_params=pltpu.CompilerParams(vmem_limit_bytes=16 * 2**20),
        cost_estimate=pl.CostEstimate(
            flops=8 * slots * tok * side * side, bytes_accessed=8 * 2**20, transcendentals=0
        ),
        name="blocks",
    )(table, x, grad_pre)


def shards(tokens, grad_act, weight_blocks, block_rows, block_cols, block_counts):
    tok, width = tokens.shape
    slots, side = weight_blocks.shape[0], weight_blocks.shape[1]
    near = lax.all_gather(tokens, "xl", axis=0, tiled=False)
    whole = lax.all_gather(near, "y", axis=0, tiled=False).reshape(FAR * NEAR, tok, width)
    table = index_table(block_rows, block_cols, block_counts, width // side)
    filled = jnp.arange(slots, dtype=jnp.int32)[:, None, None] < block_counts[0]
    weights = jnp.where(filled, weight_blocks, jnp.zeros_like(weight_blocks))
    activated, grad_pre, input_partial = hidden(
        whole, grad_act, weights, table
    )

    far_sum = lax.psum_scatter(
        input_partial.reshape(FAR, NEAR, tok, width), "y", scatter_dimension=0, tiled=True
    )[0]
    both = lax.all_gather(far_sum[1], "xl", axis=0, tiled=False)
    taken = lax.dynamic_index_in_dim(both, 1 - lax.axis_index("xl"), 0, keepdims=False)
    grad_input = (far_sum[0].astype(jnp.float32) + taken.astype(jnp.float32)).astype(jnp.bfloat16)

    keep, send = blocks(whole, grad_pre, table)
    other = lax.ppermute(send, "core", [(0, 1), (1, 0)])
    chip_sum = (keep.astype(jnp.float32) + other.astype(jnp.float32)).astype(jnp.bfloat16)
    parts = lax.all_to_all(chip_sum, ("xh", "z"), split_axis=0, concat_axis=0, tiled=True)
    parts, grad_input = lax.optimization_barrier((parts, grad_input))
    grad_blocks = jnp.sum(parts.astype(jnp.float32), axis=0)
    return (activated, grad_input, grad_blocks.reshape(slots, 4, grad_blocks.shape[-1]))


def solution(mesh):
    cut = Mesh(mesh.devices.reshape(SIZES), AXES)
    placed = (P(DP, MP), P(DP, MP), P(MP, None, None), P(MP), P(MP), P(MP))
    return jax.shard_map(
        shards,
        mesh=cut,
        in_specs=placed,
        out_specs=(P(DP, MP), P(DP, MP), P(MP, DP, None)),
        check_vma=False,
    )
```

```python
import functools

import jax
import jax.numpy as jnp
from jax import lax
from jax.experimental import pallas as pl
from jax.experimental.pallas import tpu as pltpu
from jax.sharding import Mesh, PartitionSpec as P


inv_sqrt_two = 0.7071067811865476
inv_sqrt_two_pi = 0.3989422804014327

AXES = ("xh", "z", "core", "xl", "y")
SIZES = (2, 8, 2, 2, 8)
DP = ("xh", "z", "core")
MP = ("xl", "y")
NEAR = SIZES[3]
FAR = SIZES[4]
UNROLL = 4
LARGE = 192
SMALL = 32


def cols_at(block, side):
    return (slice(None), pl.ds(pl.multiple_of(block * side, side), side))


def row_at(place, part, side):
    return (place,) + cols_at(part, side)


FROM, TO, PART, COL, LIVE, CORE = range(6)


def index_table(block_rows, block_cols, block_counts, per):
    holder = block_rows // per
    own = lax.axis_index("xl").astype(jnp.int32)
    start = (holder % FAR) * NEAR
    near = holder // FAR
    live = (jnp.arange(block_rows.shape[0], dtype=jnp.int32) < block_counts[0]).astype(jnp.int32)
    core = jnp.broadcast_to(lax.axis_index("core").astype(jnp.int32), block_rows.shape)
    return jnp.stack(
        [start + near, start + (near + own) % NEAR, block_rows % per, block_cols, live, core]
    )


def token_copies(sources, x_ref, sems):
    copies, start = [], 0
    for n, source in enumerate(sources):
        count = source.shape[1]
        target = x_ref.at[:, pl.ds(start, count), :]
        copies.append(pltpu.make_async_copy(source, target, sems.at[n]))
        start += count
    return copies


def hidden_kernel(
    table,
    *refs,
):
    pieces = len(refs) - REST
    hidden_body(table, refs[:pieces], *refs[pieces:])


REST = 19


def hidden_body(
    table,
    pieces,
    g_hbm,
    w_hbm,
    act_hbm,
    gpre_hbm,
    gin_hbm,
    x_ref,
    g_ref,
    w_ref,
    act_ref,
    gpre_ref,
    gin_ref,
    pre,
    acc,
    x_sem,
    gin_sem,
    g_sem,
    w_sem,
    act_sem,
    gpre_sem,
):
    slots, side = w_ref.shape[0], w_ref.shape[1]
    holders, tok = x_ref.shape[0], x_ref.shape[1]

    x_copies = token_copies(pieces, x_ref, x_sem)

    def gin_copy(i):
        return pltpu.make_async_copy(gin_ref.at[i], gin_hbm.at[i], gin_sem.at[i])

    g_copy = pltpu.make_async_copy(g_hbm, g_ref, g_sem)
    w_copy = pltpu.make_async_copy(w_hbm, w_ref, w_sem)
    act_copy = pltpu.make_async_copy(act_ref, act_hbm, act_sem)
    gpre_copy = pltpu.make_async_copy(gpre_ref, gpre_hbm, gpre_sem)

    w_copy.start()

    for copy in x_copies:
        copy.start()
    g_copy.start()
    pre[...] = jnp.zeros_like(pre)
    acc[...] = jnp.zeros_like(acc)
    w_copy.wait()

    for copy in x_copies:
        copy.wait()

    @pl.loop(0, slots // UNROLL)
    def _(group):
        products = []
        for k in range(UNROLL):
            s = group * UNROLL + k
            products.append(
                jnp.dot(
                    x_ref[row_at(table[FROM, s], table[PART, s], side)],
                    w_ref[s],
                    preferred_element_type=jnp.float32,
                )
            )
        for k in range(UNROLL):
            pre[cols_at(table[COL, group * UNROLL + k], side)] += products[k]

    g_copy.wait()
    step = 16

    @pl.loop(0, tok // step)
    def _(i):
        at = (pl.ds(pl.multiple_of(i * step, step), step), slice(None))
        v = pre[at]
        normal_cdf = 0.5 * (1.0 + lax.erf(v * inv_sqrt_two))
        act_ref[at] = (v * normal_cdf).astype(jnp.bfloat16)
        slopes = normal_cdf + v * jnp.exp(-0.5 * v * v) * inv_sqrt_two_pi
        gpre_ref[at] = (g_ref[at].astype(jnp.float32) * slopes).astype(jnp.bfloat16)

    act_copy.start()
    gpre_copy.start()

    @pl.loop(0, slots // UNROLL)
    def _(group):
        products = []
        for k in range(UNROLL):
            s = group * UNROLL + k
            products.append(
                lax.dot_general(
                    gpre_ref[cols_at(table[COL, s], side)],
                    w_ref[s],
                    (((1,), (1,)), ((), ())),
                    preferred_element_type=jnp.float32,
                )
            )
        for k in range(UNROLL):
            s = group * UNROLL + k
            acc[row_at(table[TO, s], table[PART, s], side)] += products[k]

    @pl.loop(0, holders)
    def _(i):
        gin_ref[i] = acc[i].astype(jnp.bfloat16)
        gin_copy(i).start()

    act_copy.wait()
    gpre_copy.wait()

    @pl.loop(0, holders)
    def _(i):
        gin_copy(i).wait()


def hidden(pieces, grad_act, weights, table):
    holders, _, width = pieces[0].shape
    tok, ff = grad_act.shape
    slots, side, _ = weights.shape
    hbm = pl.BlockSpec(memory_space=pltpu.HBM)
    narrow = jnp.bfloat16
    return pl.pallas_call(
        hidden_kernel,
        grid_spec=pltpu.PrefetchScalarGridSpec(
            num_scalar_prefetch=1,
            grid=(),
            in_specs=[hbm] * (len(pieces) + 2),
            out_specs=[hbm] * 3,
            scratch_shapes=[
                pltpu.VMEM((holders, tok, width), narrow),
                pltpu.VMEM((tok, ff), narrow),
                pltpu.VMEM((slots, side, side), narrow),
                pltpu.VMEM((tok, ff), narrow),
                pltpu.VMEM((tok, ff), narrow),
                pltpu.VMEM((holders, tok, width), narrow),
                pltpu.VMEM((tok, ff), jnp.float32),
                pltpu.VMEM((holders, tok, width), jnp.float32),
                pltpu.SemaphoreType.DMA((len(pieces),)),
                pltpu.SemaphoreType.DMA((holders,)),
                pltpu.SemaphoreType.DMA,
                pltpu.SemaphoreType.DMA,
                pltpu.SemaphoreType.DMA,
                pltpu.SemaphoreType.DMA,
            ],
        ),
        out_shape=[
            jax.ShapeDtypeStruct((tok, ff), narrow),
            jax.ShapeDtypeStruct((tok, ff), narrow),
            jax.ShapeDtypeStruct((holders, tok, width), narrow),
        ],
        compiler_params=pltpu.CompilerParams(vmem_limit_bytes=60 * 2**20),
        cost_estimate=pl.CostEstimate(
            flops=4 * slots * tok * side * side,
            bytes_accessed=12 * 2**20,
            transcendentals=2 * tok * ff,
        ),
        name="hidden",
    )(table, *pieces, grad_act, weights)


def blocks_kernel(table, *refs):
    pieces = len(refs) - 7
    blocks_body(table, refs[:pieces], *refs[pieces:])


def blocks_body(
    table, pieces, gpre_hbm, keep_ref, send_ref, x_ref, gpre_ref, x_sem, gpre_sem
):
    x_copies = token_copies(pieces, x_ref, x_sem)
    gpre_copy = pltpu.make_async_copy(gpre_hbm, gpre_ref, gpre_sem)
    for copy in x_copies:
        copy.start()
    gpre_copy.start()
    side = gpre_ref.shape[0] // 2
    slots = table.shape[1]
    groups = keep_ref.shape[0]
    to = lax.broadcasted_iota(jnp.int32, (2 * side, 2 * side), 0)
    source = lax.broadcasted_iota(jnp.int32, (2 * side, 2 * side), 1)
    core = (to // side + table[CORE, 0]) % 2
    wanted = ((to % 8) // 4) * side + ((to % side) // 8 * 2 + core) * 4 + to % 4
    pick = (source == wanted).astype(jnp.float32).astype(jnp.bfloat16)
    for copy in x_copies:
        copy.wait()
    gpre_copy.wait()

    @pl.loop(0, slots // UNROLL)
    def _(group):
        for h in range(UNROLL // 2):
            pair = []
            for k in range(2):
                s = group * UNROLL + h * 2 + k
                value = lax.dot_general(
                    x_ref[row_at(table[FROM, s], table[PART, s], side)],
                    gpre_ref[cols_at(table[COL, s], side)],
                    (((0,), (0,)), ((), ())),
                    preferred_element_type=jnp.float32,
                )
                pair.append(jnp.where(table[LIVE, s] > 0, value, 0.0).astype(jnp.bfloat16))
            both = jnp.dot(pick, jnp.concatenate(pair, 0), preferred_element_type=jnp.float32)
            both = both.astype(jnp.bfloat16).reshape(2, groups, 8, side)
            keep_ref[:, group * (UNROLL // 2) + h] = both[0]
            send_ref[:, group * (UNROLL // 2) + h] = both[1]


def blocks(pieces, grad_pre, table):
    slots = table.shape[1]
    holders, _, width = pieces[0].shape
    tok = grad_pre.shape[0]
    side = tok // 2
    hbm = pl.BlockSpec(memory_space=pltpu.HBM)
    half = jax.ShapeDtypeStruct((SIZES[0] * SIZES[1], slots // 2, 8, side), jnp.bfloat16)
    vmem = pl.BlockSpec(memory_space=pltpu.VMEM)
    return pl.pallas_call(
        blocks_kernel,
        grid_spec=pltpu.PrefetchScalarGridSpec(
            num_scalar_prefetch=1,
            grid=(),
            in_specs=[hbm] * (len(pieces) + 1),
            out_specs=[vmem] * 2,
            scratch_shapes=[
                pltpu.VMEM((holders, tok, width), jnp.bfloat16),
                pltpu.VMEM(grad_pre.shape, jnp.bfloat16),
                pltpu.SemaphoreType.DMA((len(pieces),)),
                pltpu.SemaphoreType.DMA,
            ],
        ),
        out_shape=[half, half],
        compiler_params=pltpu.CompilerParams(vmem_limit_bytes=58 * 2**20),
        cost_estimate=pl.CostEstimate(
            flops=8 * slots * tok * side * side, bytes_accessed=8 * 2**20, transcendentals=0
        ),
        name="blocks",
    )(table, *pieces, grad_pre)


def shards(tokens, grad_act, weight_blocks, block_rows, block_cols, block_counts):
    tok, width = tokens.shape
    slots, side = weight_blocks.shape[0], weight_blocks.shape[1]
    large = lax.all_gather(tokens[:LARGE], "xl", axis=0, tiled=False)
    whole = [lax.all_gather(large, "y", axis=0, tiled=False).reshape(FAR * NEAR, LARGE, width)]
    for start in range(LARGE, tok, SMALL):
        small = lax.all_gather(tokens[start : start + SMALL], "xl", axis=0, tiled=False)
        small = lax.all_gather(small, "y", axis=0, tiled=False)
        whole.append(small.reshape(FAR * NEAR, SMALL, width))
    table = index_table(block_rows, block_cols, block_counts, width // side)
    filled = jnp.arange(slots, dtype=jnp.int32)[:, None, None] < block_counts[0]
    weights = jnp.where(filled, weight_blocks, jnp.zeros_like(weight_blocks))
    activated, grad_pre, input_partial = hidden(
        whole, grad_act, weights, table
    )

    far_sum = lax.psum_scatter(
        input_partial.reshape(FAR, NEAR, tok, width), "y", scatter_dimension=0, tiled=True
    )[0]
    both = lax.all_gather(far_sum[1], "xl", axis=0, tiled=False)
    taken = jnp.where(lax.axis_index("xl") == 0, both[1], both[0])
    grad_input = (far_sum[0].astype(jnp.float32) + taken.astype(jnp.float32)).astype(jnp.bfloat16)

    keep, send = blocks(whole, grad_pre, table)
    other = lax.ppermute(send, "core", [(0, 1), (1, 0)])
    chip_sum = (keep.astype(jnp.float32) + other.astype(jnp.float32)).astype(jnp.bfloat16)
    parts = lax.all_to_all(chip_sum, ("xh", "z"), split_axis=0, concat_axis=0, tiled=True)
    parts, grad_input = lax.optimization_barrier((parts, grad_input))
    grad_blocks = jnp.sum(parts.astype(jnp.float32), axis=0)
    return (activated, grad_input, grad_blocks.reshape(slots, 4, grad_blocks.shape[-1]))


def solution(mesh):
    cut = Mesh(mesh.devices.reshape(SIZES), AXES)
    placed = (P(DP, MP), P(DP, MP), P(MP, None, None), P(MP), P(MP), P(MP))
    return jax.shard_map(
        shards,
        mesh=cut,
        in_specs=placed,
        out_specs=(P(DP, MP), P(DP, MP), P(MP, DP, None)),
        check_vma=False,
    )
```

```python
import functools

import jax
import jax.numpy as jnp
from jax import lax
from jax.experimental import pallas as pl
from jax.experimental.pallas import tpu as pltpu
from jax.sharding import Mesh, PartitionSpec as P


inv_sqrt_two = 0.7071067811865476
inv_sqrt_two_pi = 0.3989422804014327

AXES = ("xh", "z", "core", "xl", "y")
SIZES = (2, 8, 2, 2, 8)
DP = ("xh", "z", "core")
MP = ("xl", "y")
NEAR = SIZES[3]
FAR = SIZES[4]
UNROLL = 32
PAIRS = 19


def cols_at(block, side):
    return (slice(None), pl.ds(pl.multiple_of(block * side, side), side))


def row_at(place, part, side):
    return (place,) + cols_at(part, side)


FROM, PART, COL, LIVE, CORE = range(5)


def index_table(block_rows, block_cols, block_counts, per):
    holder = block_rows // per
    place = (holder % FAR) * NEAR + holder // FAR
    live = (jnp.arange(block_rows.shape[0], dtype=jnp.int32) < block_counts[0]).astype(jnp.int32)
    core = jnp.broadcast_to(lax.axis_index("core").astype(jnp.int32), block_rows.shape)
    return jnp.stack([place, block_rows % per, block_cols, live, core])


PAIR_COL, PAIR_SLOTS = 0, (1, 5)


def pair_table(block_rows, block_cols, block_counts, per, columns):
    slots = block_rows.shape[0]
    pairs = (slots + columns) // 2
    ids = jnp.arange(slots, dtype=jnp.int32)
    live = ids < block_counts[0]
    same = (block_cols[:, None] == block_cols[None, :]) & live[None, :] & (ids[None, :] < ids[:, None])
    rank = jnp.sum(same.astype(jnp.int32), axis=1)
    column = jnp.arange(columns, dtype=jnp.int32)
    used = jnp.sum(((block_cols[None, :] == column[:, None]) & live[None, :]).astype(jnp.int32), axis=1)
    before = column[None, :] < block_cols[:, None]
    pair = jnp.sum(jnp.where(before, (used[None, :] + 1) // 2, 0), axis=1) + rank // 2
    holder = block_rows // per
    own = lax.axis_index("xl").astype(jnp.int32)
    start = (holder % FAR) * NEAR
    near = holder // FAR
    number = jnp.arange(pairs, dtype=jnp.int32)[:, None]
    lines = []
    for place in range(2):
        hot = (pair[None, :] == number) & (rank % 2 == place)[None, :] & live[None, :]

        def chosen(values):
            return jnp.sum(jnp.where(hot, values[None, :], 0), axis=1)

        if place == 0:
            lines.append(chosen(block_cols))
        lines.append(slots + chosen(ids - slots))
        lines.append(chosen(start + near))
        lines.append(chosen(start + (near + own) % NEAR))
        lines.append(chosen(block_rows % per))
    return jnp.stack(lines)


def hidden_kernel(
    table,
    x_hbm,
    g_hbm,
    w_hbm,
    act_hbm,
    gpre_hbm,
    gin_hbm,
    x_ref,
    g_ref,
    w_ref,
    act_ref,
    gpre_ref,
    gin_ref,
    pre,
    acc,
    x_sem,
    gin_sem,
    g_sem,
    w_sem,
    act_sem,
    gpre_sem,
):
    slots, side = w_hbm.shape[0], w_ref.shape[1]
    pairs = table.shape[1]
    holders, tok = x_ref.shape[0], x_ref.shape[1]

    def x_copy(i):
        return pltpu.make_async_copy(x_hbm.at[i], x_ref.at[i], x_sem.at[i])

    def gin_copy(i):
        return pltpu.make_async_copy(gin_ref.at[i], gin_hbm.at[i], gin_sem.at[i])

    g_copy = pltpu.make_async_copy(g_hbm, g_ref, g_sem)
    w_copy = pltpu.make_async_copy(w_hbm, w_ref.at[pl.ds(0, slots)], w_sem)
    act_copy = pltpu.make_async_copy(act_ref, act_hbm, act_sem)
    gpre_copy = pltpu.make_async_copy(gpre_ref, gpre_hbm, gpre_sem)

    w_copy.start()

    @pl.loop(0, holders)
    def _(i):
        x_copy(i).start()

    g_copy.start()
    w_ref[slots] = jnp.zeros((side, side), w_ref.dtype)
    pre[...] = jnp.zeros_like(pre)
    acc[...] = jnp.zeros_like(acc)
    w_copy.wait()

    @pl.loop(0, holders)
    def _(i):
        x_copy(i).wait()

    def weights_of(number):
        first, second = (w_ref[table[row, number]] for row in PAIR_SLOTS)
        return jnp.concatenate([first, second], axis=0)

    @pl.loop(0, pairs // PAIRS)
    def _(group):
        products = []
        for k in range(PAIRS):
            number = group * PAIRS + k
            both = [
                x_ref[row_at(table[row + 1, number], table[row + 3, number], side)]
                for row in PAIR_SLOTS
            ]
            products.append(
                jnp.dot(
                    jnp.concatenate(both, axis=1),
                    weights_of(number),
                    preferred_element_type=jnp.float32,
                )
            )
        for k in range(PAIRS):
            pre[cols_at(table[PAIR_COL, group * PAIRS + k], side)] += products[k]

    g_copy.wait()
    step = 16

    @pl.loop(0, tok // step)
    def _(i):
        at = (pl.ds(pl.multiple_of(i * step, step), step), slice(None))
        v = pre[at]
        normal_cdf = 0.5 * (1.0 + lax.erf(v * inv_sqrt_two))
        act_ref[at] = (v * normal_cdf).astype(jnp.bfloat16)
        slopes = normal_cdf + v * jnp.exp(-0.5 * v * v) * inv_sqrt_two_pi
        gpre_ref[at] = (g_ref[at].astype(jnp.float32) * slopes).astype(jnp.bfloat16)

    act_copy.start()
    gpre_copy.start()

    @pl.loop(0, pairs // PAIRS)
    def _(group):
        products = []
        for k in range(PAIRS):
            number = group * PAIRS + k
            products.append(
                lax.dot_general(
                    gpre_ref[cols_at(table[PAIR_COL, number], side)],
                    weights_of(number),
                    (((1,), (1,)), ((), ())),
                    preferred_element_type=jnp.float32,
                )
            )
        for k in range(PAIRS):
            number = group * PAIRS + k
            for n, row in enumerate(PAIR_SLOTS):
                at = row_at(table[row + 2, number], table[row + 3, number], side)
                acc[at] += products[k][:, n * side : (n + 1) * side]

    @pl.loop(0, holders)
    def _(i):
        gin_ref[i] = acc[i].astype(jnp.bfloat16)
        gin_copy(i).start()

    act_copy.wait()
    gpre_copy.wait()

    @pl.loop(0, holders)
    def _(i):
        gin_copy(i).wait()


def hidden(x, grad_act, weights, table):
    holders, tok, width = x.shape
    ff = grad_act.shape[1]
    slots, side, _ = weights.shape
    hbm = pl.BlockSpec(memory_space=pltpu.HBM)
    narrow = jnp.bfloat16
    return pl.pallas_call(
        hidden_kernel,
        grid_spec=pltpu.PrefetchScalarGridSpec(
            num_scalar_prefetch=1,
            grid=(),
            in_specs=[hbm] * 3,
            out_specs=[hbm] * 3,
            scratch_shapes=[
                pltpu.VMEM((holders, tok, width), narrow),
                pltpu.VMEM((tok, ff), narrow),
                pltpu.VMEM((slots + 1, side, side), narrow),
                pltpu.VMEM((tok, ff), narrow),
                pltpu.VMEM((tok, ff), narrow),
                pltpu.VMEM((holders, tok, width), narrow),
                pltpu.VMEM((tok, ff), jnp.float32),
                pltpu.VMEM((holders, tok, width), jnp.float32),
                pltpu.SemaphoreType.DMA((holders,)),
                pltpu.SemaphoreType.DMA((holders,)),
                pltpu.SemaphoreType.DMA,
                pltpu.SemaphoreType.DMA,
                pltpu.SemaphoreType.DMA,
                pltpu.SemaphoreType.DMA,
            ],
        ),
        out_shape=[
            jax.ShapeDtypeStruct((tok, ff), narrow),
            jax.ShapeDtypeStruct((tok, ff), narrow),
            jax.ShapeDtypeStruct((holders, tok, width), narrow),
        ],
        compiler_params=pltpu.CompilerParams(vmem_limit_bytes=60 * 2**20),
        cost_estimate=pl.CostEstimate(
            flops=4 * slots * tok * side * side,
            bytes_accessed=12 * 2**20,
            transcendentals=2 * tok * ff,
        ),
        name="hidden",
    )(table, x, grad_act, weights)


def blocks_kernel(table, x_ref, gpre_ref, keep_ref, send_ref):
    side = gpre_ref.shape[0] // 2
    slots = table.shape[1]
    groups = keep_ref.shape[0]
    to = lax.broadcasted_iota(jnp.int32, (2 * side, 2 * side), 0)
    source = lax.broadcasted_iota(jnp.int32, (2 * side, 2 * side), 1)
    core = (to // side + table[CORE, 0]) % 2
    wanted = ((to % 8) // 4) * side + ((to % side) // 8 * 2 + core) * 4 + to % 4
    pick = (source == wanted).astype(jnp.float32).astype(jnp.bfloat16)

    @pl.loop(0, slots // UNROLL)
    def _(group):
        for h in range(UNROLL // 2):
            pair = []
            for k in range(2):
                s = group * UNROLL + h * 2 + k
                value = lax.dot_general(
                    x_ref[row_at(table[FROM, s], table[PART, s], side)],
                    gpre_ref[cols_at(table[COL, s], side)],
                    (((0,), (0,)), ((), ())),
                    preferred_element_type=jnp.float32,
                )
                pair.append(jnp.where(table[LIVE, s] > 0, value, 0.0).astype(jnp.bfloat16))
            both = jnp.dot(pick, jnp.concatenate(pair, 0), preferred_element_type=jnp.float32)
            both = both.astype(jnp.bfloat16).reshape(2, groups, 8, side)
            keep_ref[:, group * (UNROLL // 2) + h] = both[0]
            send_ref[:, group * (UNROLL // 2) + h] = both[1]


def blocks(x, grad_pre, table):
    slots = table.shape[1]
    tok = x.shape[1]
    side = tok // 2
    half = jax.ShapeDtypeStruct((SIZES[0] * SIZES[1], slots // 2, 8, side), jnp.bfloat16)
    vmem = pl.BlockSpec(memory_space=pltpu.VMEM)
    return pl.pallas_call(
        blocks_kernel,
        grid_spec=pltpu.PrefetchScalarGridSpec(
            num_scalar_prefetch=1,
            grid=(),
            in_specs=[vmem] * 2,
            out_specs=[vmem] * 2,
        ),
        out_shape=[half, half],
        compiler_params=pltpu.CompilerParams(vmem_limit_bytes=16 * 2**20),
        cost_estimate=pl.CostEstimate(
            flops=8 * slots * tok * side * side, bytes_accessed=8 * 2**20, transcendentals=0
        ),
        name="blocks",
    )(table, x, grad_pre)


def shards(tokens, grad_act, weight_blocks, block_rows, block_cols, block_counts):
    tok, width = tokens.shape
    slots, side = weight_blocks.shape[0], weight_blocks.shape[1]
    near = lax.all_gather(tokens, "xl", axis=0, tiled=False)
    whole = lax.all_gather(near, "y", axis=0, tiled=False).reshape(FAR * NEAR, tok, width)
    table = index_table(block_rows, block_cols, block_counts, width // side)
    columns = grad_act.shape[1] // side
    pairs = pair_table(block_rows, block_cols, block_counts, width // side, columns)
    activated, grad_pre, input_partial = hidden(
        whole, grad_act, weight_blocks, pairs
    )

    far_sum = lax.psum_scatter(
        input_partial.reshape(FAR, NEAR, tok, width), "y", scatter_dimension=0, tiled=True
    )[0]
    both = lax.all_gather(far_sum[1], "xl", axis=0, tiled=False)
    taken = lax.dynamic_index_in_dim(both, 1 - lax.axis_index("xl"), 0, keepdims=False)
    grad_input = (far_sum[0].astype(jnp.float32) + taken.astype(jnp.float32)).astype(jnp.bfloat16)

    keep, send = blocks(whole, grad_pre, table)
    other = lax.ppermute(send, "core", [(0, 1), (1, 0)])
    chip_sum = (keep.astype(jnp.float32) + other.astype(jnp.float32)).astype(jnp.bfloat16)
    parts = lax.all_to_all(chip_sum, ("xh", "z"), split_axis=0, concat_axis=0, tiled=True)
    parts, grad_input = lax.optimization_barrier((parts, grad_input))
    grad_blocks = jnp.sum(parts.astype(jnp.float32), axis=0)
    return (activated, grad_input, grad_blocks.reshape(slots, 4, grad_blocks.shape[-1]))


def solution(mesh):
    cut = Mesh(mesh.devices.reshape(SIZES), AXES)
    placed = (P(DP, MP), P(DP, MP), P(MP, None, None), P(MP), P(MP), P(MP))
    return jax.shard_map(
        shards,
        mesh=cut,
        in_specs=placed,
        out_specs=(P(DP, MP), P(DP, MP), P(MP, DP, None)),
        check_vma=False,
    )
```

```python
import functools

import jax
import jax.numpy as jnp
from jax import lax
from jax.experimental import pallas as pl
from jax.experimental.pallas import tpu as pltpu
from jax.sharding import Mesh, PartitionSpec as P


inv_sqrt_two = 0.7071067811865476
inv_sqrt_two_pi = 0.3989422804014327

AXES = ("xh", "z", "core", "xl", "y")
SIZES = (2, 8, 2, 2, 8)
DP = ("xh", "z", "core")
MP = ("xl", "y")
NEAR = SIZES[3]
FAR = SIZES[4]
UNROLL = 32
PAIRS = 19


def cols_at(block, side):
    return (slice(None), pl.ds(pl.multiple_of(block * side, side), side))


def row_at(place, part, side):
    return (place,) + cols_at(part, side)


FROM, PART, COL, LIVE, CORE = range(5)


def index_table(block_rows, block_cols, block_counts, per):
    holder = block_rows // per
    place = (holder % FAR) * NEAR + holder // FAR
    live = (jnp.arange(block_rows.shape[0], dtype=jnp.int32) < block_counts[0]).astype(jnp.int32)
    core = jnp.broadcast_to(lax.axis_index("core").astype(jnp.int32), block_rows.shape)
    return jnp.stack([place, block_rows % per, block_cols, live, core])


PAIR_COL, PAIR_SLOTS = 0, (1, 4)


def pair_table(block_rows, block_cols, block_counts, per, columns):
    slots = block_rows.shape[0]
    pairs = (slots + columns) // 2
    ids = jnp.arange(slots, dtype=jnp.int32)
    live = ids < block_counts[0]
    same = (block_cols[:, None] == block_cols[None, :]) & live[None, :] & (ids[None, :] < ids[:, None])
    rank = jnp.sum(same.astype(jnp.int32), axis=1)
    column = jnp.arange(columns, dtype=jnp.int32)
    used = jnp.sum(((block_cols[None, :] == column[:, None]) & live[None, :]).astype(jnp.int32), axis=1)
    before = column[None, :] < block_cols[:, None]
    pair = jnp.sum(jnp.where(before, (used[None, :] + 1) // 2, 0), axis=1) + rank // 2
    holder = block_rows // per
    start = (holder % FAR) * NEAR
    near = holder // FAR
    number = jnp.arange(pairs, dtype=jnp.int32)[:, None]
    lines = []
    for place in range(2):
        hot = (pair[None, :] == number) & (rank % 2 == place)[None, :] & live[None, :]

        def chosen(values):
            return jnp.sum(jnp.where(hot, values[None, :], 0), axis=1)

        if place == 0:
            lines.append(chosen(block_cols))
        lines.append(slots + chosen(ids - slots))
        lines.append(chosen(start + near))
        lines.append(chosen(block_rows % per))
    return jnp.stack(lines)


def hidden_kernel(
    table,
    x_hbm,
    g_hbm,
    w_hbm,
    act_hbm,
    gpre_hbm,
    gin_hbm,
    x_ref,
    g_ref,
    w_ref,
    act_ref,
    gpre_ref,
    gin_ref,
    pre,
    acc,
    x_sem,
    gin_sem,
    g_sem,
    w_sem,
    act_sem,
    gpre_sem,
):
    slots, side = w_hbm.shape[0], w_ref.shape[1]
    pairs = table.shape[1]
    holders, tok = x_ref.shape[0], x_ref.shape[1]

    def x_copy(i):
        return pltpu.make_async_copy(x_hbm.at[i], x_ref.at[i], x_sem.at[i])

    def gin_copy(i):
        return pltpu.make_async_copy(gin_ref.at[i], gin_hbm.at[i], gin_sem.at[i])

    g_copy = pltpu.make_async_copy(g_hbm, g_ref, g_sem)
    w_copy = pltpu.make_async_copy(w_hbm, w_ref.at[pl.ds(0, slots)], w_sem)
    act_copy = pltpu.make_async_copy(act_ref, act_hbm, act_sem)
    gpre_copy = pltpu.make_async_copy(gpre_ref, gpre_hbm, gpre_sem)

    w_copy.start()

    @pl.loop(0, holders)
    def _(i):
        x_copy(i).start()

    g_copy.start()
    w_ref[slots] = jnp.zeros((side, side), w_ref.dtype)
    pre[...] = jnp.zeros_like(pre)
    acc[...] = jnp.zeros_like(acc)
    w_copy.wait()

    @pl.loop(0, holders)
    def _(i):
        x_copy(i).wait()

    def weights_of(number):
        first, second = (w_ref[table[row, number]] for row in PAIR_SLOTS)
        return jnp.concatenate([first, second], axis=0)

    @pl.loop(0, pairs // PAIRS)
    def _(group):
        products = []
        for k in range(PAIRS):
            number = group * PAIRS + k
            both = [
                x_ref[row_at(table[row + 1, number], table[row + 2, number], side)]
                for row in PAIR_SLOTS
            ]
            products.append(
                jnp.dot(
                    jnp.concatenate(both, axis=1),
                    weights_of(number),
                    preferred_element_type=jnp.float32,
                )
            )
        for k in range(PAIRS):
            pre[cols_at(table[PAIR_COL, group * PAIRS + k], side)] += products[k]

    g_copy.wait()
    step = 16

    @pl.loop(0, tok // step)
    def _(i):
        at = (pl.ds(pl.multiple_of(i * step, step), step), slice(None))
        v = pre[at]
        normal_cdf = 0.5 * (1.0 + lax.erf(v * inv_sqrt_two))
        act_ref[at] = (v * normal_cdf).astype(jnp.bfloat16)
        slopes = normal_cdf + v * jnp.exp(-0.5 * v * v) * inv_sqrt_two_pi
        gpre_ref[at] = (g_ref[at].astype(jnp.float32) * slopes).astype(jnp.bfloat16)

    act_copy.start()
    gpre_copy.start()

    @pl.loop(0, pairs // PAIRS)
    def _(group):
        products = []
        for k in range(PAIRS):
            number = group * PAIRS + k
            products.append(
                lax.dot_general(
                    gpre_ref[cols_at(table[PAIR_COL, number], side)],
                    weights_of(number),
                    (((1,), (1,)), ((), ())),
                    preferred_element_type=jnp.float32,
                )
            )
        for k in range(PAIRS):
            number = group * PAIRS + k
            for n, row in enumerate(PAIR_SLOTS):
                at = row_at(table[row + 1, number], table[row + 2, number], side)
                acc[at] += products[k][:, n * side : (n + 1) * side]

    @pl.loop(0, holders)
    def _(i):
        gin_ref[i] = acc[i].astype(jnp.bfloat16)
        gin_copy(i).start()

    act_copy.wait()
    gpre_copy.wait()

    @pl.loop(0, holders)
    def _(i):
        gin_copy(i).wait()


def hidden(x, grad_act, weights, table):
    holders, tok, width = x.shape
    ff = grad_act.shape[1]
    slots, side, _ = weights.shape
    hbm = pl.BlockSpec(memory_space=pltpu.HBM)
    narrow = jnp.bfloat16
    return pl.pallas_call(
        hidden_kernel,
        grid_spec=pltpu.PrefetchScalarGridSpec(
            num_scalar_prefetch=1,
            grid=(),
            in_specs=[hbm] * 3,
            out_specs=[hbm] * 3,
            scratch_shapes=[
                pltpu.VMEM((holders, tok, width), narrow),
                pltpu.VMEM((tok, ff), narrow),
                pltpu.VMEM((slots + 1, side, side), narrow),
                pltpu.VMEM((tok, ff), narrow),
                pltpu.VMEM((tok, ff), narrow),
                pltpu.VMEM((holders, tok, width), narrow),
                pltpu.VMEM((tok, ff), jnp.float32),
                pltpu.VMEM((holders, tok, width), jnp.float32),
                pltpu.SemaphoreType.DMA((holders,)),
                pltpu.SemaphoreType.DMA((holders,)),
                pltpu.SemaphoreType.DMA,
                pltpu.SemaphoreType.DMA,
                pltpu.SemaphoreType.DMA,
                pltpu.SemaphoreType.DMA,
            ],
        ),
        out_shape=[
            jax.ShapeDtypeStruct((tok, ff), narrow),
            jax.ShapeDtypeStruct((tok, ff), narrow),
            jax.ShapeDtypeStruct((holders, tok, width), narrow),
        ],
        compiler_params=pltpu.CompilerParams(vmem_limit_bytes=60 * 2**20),
        cost_estimate=pl.CostEstimate(
            flops=4 * slots * tok * side * side,
            bytes_accessed=12 * 2**20,
            transcendentals=2 * tok * ff,
        ),
        name="hidden",
    )(table, x, grad_act, weights)


def blocks_kernel(table, x_ref, gpre_ref, keep_ref, send_ref):
    side = gpre_ref.shape[0] // 2
    slots = table.shape[1]
    groups = keep_ref.shape[0]
    to = lax.broadcasted_iota(jnp.int32, (2 * side, 2 * side), 0)
    source = lax.broadcasted_iota(jnp.int32, (2 * side, 2 * side), 1)
    core = (to // side + table[CORE, 0]) % 2
    wanted = ((to % 8) // 4) * side + ((to % side) // 8 * 2 + core) * 4 + to % 4
    pick = (source == wanted).astype(jnp.float32).astype(jnp.bfloat16)

    @pl.loop(0, slots // UNROLL)
    def _(group):
        for h in range(UNROLL // 2):
            pair = []
            for k in range(2):
                s = group * UNROLL + h * 2 + k
                value = lax.dot_general(
                    x_ref[row_at(table[FROM, s], table[PART, s], side)],
                    gpre_ref[cols_at(table[COL, s], side)],
                    (((0,), (0,)), ((), ())),
                    preferred_element_type=jnp.float32,
                )
                pair.append(jnp.where(table[LIVE, s] > 0, value, 0.0).astype(jnp.bfloat16))
            both = jnp.dot(pick, jnp.concatenate(pair, 0), preferred_element_type=jnp.float32)
            both = both.astype(jnp.bfloat16).reshape(2, groups, 8, side)
            keep_ref[:, group * (UNROLL // 2) + h] = both[0]
            send_ref[:, group * (UNROLL // 2) + h] = both[1]


def blocks(x, grad_pre, table):
    slots = table.shape[1]
    tok = x.shape[1]
    side = tok // 2
    half = jax.ShapeDtypeStruct((SIZES[0] * SIZES[1], slots // 2, 8, side), jnp.bfloat16)
    vmem = pl.BlockSpec(memory_space=pltpu.VMEM)
    return pl.pallas_call(
        blocks_kernel,
        grid_spec=pltpu.PrefetchScalarGridSpec(
            num_scalar_prefetch=1,
            grid=(),
            in_specs=[vmem] * 2,
            out_specs=[vmem] * 2,
        ),
        out_shape=[half, half],
        compiler_params=pltpu.CompilerParams(vmem_limit_bytes=16 * 2**20),
        cost_estimate=pl.CostEstimate(
            flops=8 * slots * tok * side * side, bytes_accessed=8 * 2**20, transcendentals=0
        ),
        name="blocks",
    )(table, x, grad_pre)


def shards(tokens, grad_act, weight_blocks, block_rows, block_cols, block_counts):
    tok, width = tokens.shape
    slots, side = weight_blocks.shape[0], weight_blocks.shape[1]
    near = lax.all_gather(tokens, "xl", axis=0, tiled=False)
    whole = lax.all_gather(near, "y", axis=0, tiled=False).reshape(FAR * NEAR, tok, width)
    table = index_table(block_rows, block_cols, block_counts, width // side)
    columns = grad_act.shape[1] // side
    pairs = pair_table(block_rows, block_cols, block_counts, width // side, columns)
    activated, grad_pre, input_partial = hidden(
        whole, grad_act, weight_blocks, pairs
    )

    far_sum = lax.psum_scatter(
        input_partial.reshape(FAR, NEAR, tok, width), "y", scatter_dimension=0, tiled=True
    )[0]
    halves = lax.all_to_all(far_sum, "xl", split_axis=0, concat_axis=0, tiled=True)
    grad_input = jnp.sum(halves.astype(jnp.float32), axis=0).astype(jnp.bfloat16)

    keep, send = blocks(whole, grad_pre, table)
    other = lax.ppermute(send, "core", [(0, 1), (1, 0)])
    chip_sum = (keep.astype(jnp.float32) + other.astype(jnp.float32)).astype(jnp.bfloat16)
    parts = lax.all_to_all(chip_sum, ("xh", "z"), split_axis=0, concat_axis=0, tiled=True)
    parts, far_sum = lax.optimization_barrier((parts, far_sum))
    grad_blocks = jnp.sum(parts.astype(jnp.float32), axis=0)
    return (activated, grad_input, grad_blocks.reshape(slots, 4, grad_blocks.shape[-1]))


def solution(mesh):
    cut = Mesh(mesh.devices.reshape(SIZES), AXES)
    placed = (P(DP, MP), P(DP, MP), P(MP, None, None), P(MP), P(MP), P(MP))
    return jax.shard_map(
        shards,
        mesh=cut,
        in_specs=placed,
        out_specs=(P(DP, MP), P(DP, MP), P(MP, DP, None)),
        check_vma=False,
    )
```
